256 devices in a mesh: member: 128 (over y, z, x), pair: 2 (over core).
Axes of the slice: x: 4, y: 4, z: 8, core: 2. Of those that a mesh axis runs over, the one named last changes fastest.
Arguments:
- samples: bfloat16 [512, 512], replicated, may hold values from -6 to 6
- w_first: bfloat16 [128, 512, 2048], P('member', None, 'pair'), may hold values from -6 to 6
- b_first: bfloat16 [128, 2048], P('member', 'pair'), may hold values from -6 to 6
- w_second: bfloat16 [128, 2048, 2048], P('member', None, 'pair'), may hold values from -6 to 6
- b_second: bfloat16 [128, 2048], P('member', 'pair'), may hold values from -6 to 6
- w_third: bfloat16 [128, 2048, 64], P('member', 'pair'), may hold values from -6 to 6
- observed: float32 [512, 64], replicated, may hold values from -24 to 24
- perturb: float32 [128, 512, 64], P('member'), may hold values from -6 to 6
- variance: float32 [512, 64], replicated, may hold values from 32 to 1024
Outputs:
- new_first: bfloat16 [128, 512, 2048], P('member', None, 'pair')
- new_bfirst: bfloat16 [128, 2048], P('member', 'pair')
- new_second: bfloat16 [128, 2048, 2048], P('member', None, 'pair')
- new_bsecond: bfloat16 [128, 2048], P('member', 'pair')
- new_third: bfloat16 [128, 2048, 64], P('member', 'pair')
The draws below stay inside these ranges and needn't reach their ends.
All inputs are finite; a program needn't handle non-finite values.
Results may differ from the reference program's by a relative error of at most 0.019.
Values may be sent and summed in bfloat16 or wider, within the bound.
A program may use at most 128 MiB of HBM per device.

```python
import math
import jax
import jax.numpy as jnp
from jax import lax

IN = 512
H = 2048
OUT = 64
S = 512
MEMBERS = 128


def block_levels(rng, dims, shards, smallest, high):
    level = 1.0
    for axis_at, parts in shards:
        draws = jax.random.uniform(jax.random.fold_in(jax.random.fold_in(rng, 6), axis_at), (parts,), jnp.float32, smallest / len(shards), high / len(shards))
        level = level * jnp.repeat(jnp.exp(draws), dims[axis_at] // parts).reshape((-1,) + (1,) * (len(dims) - 1 - axis_at))
    return level


def gaussian(rng, extent, scale, bound, split=(), kind=jnp.bfloat16):
    entries = jax.random.normal(rng, extent, jnp.float32) * scale
    if len(split) > 0:
        entries = block_levels(rng, extent, split, -0.22, 0.18) * entries
    return jnp.clip(entries, min=-bound, max=bound).astype(kind)


def setup_inputs(seed: int = 0) -> dict:
    arg_keys = jax.random.split(jax.random.key(seed), 10)
    samples = gaussian(arg_keys[0], (S, IN), 1.0, 6.0)
    w_first = gaussian(arg_keys[1], (MEMBERS, IN, H), 1.0, 6.0, ((0, 128), (2, 2)))
    b_first = gaussian(arg_keys[2], (MEMBERS, H), 1.0, 6.0, ((0, 128), (1, 2)))
    w_second = gaussian(arg_keys[3], (MEMBERS, H, H), 1.0, 6.0, ((0, 128), (2, 2)))
    b_second = gaussian(arg_keys[4], (MEMBERS, H), 1.0, 6.0, ((0, 128), (1, 2)))
    w_third = gaussian(arg_keys[5], (MEMBERS, H, OUT), 1.0, 6.0, ((0, 128), (1, 2)))
    observed = gaussian(arg_keys[6], (S, OUT), 4.0, 24.0, (), jnp.float32)
    perturb = gaussian(arg_keys[7], (MEMBERS, S, OUT), 1.0, 6.0, ((0, 128),), jnp.float32)
    variance = jnp.clip(jnp.exp(jax.random.uniform(arg_keys[8], (S, OUT), jnp.float32, math.log(32.0), math.log(1024.0))), 32.0, 1024.0)
    return dict(samples=samples, w_first=w_first, b_first=b_first, w_second=w_second, b_second=b_second, w_third=w_third, observed=observed, perturb=perturb, variance=variance)


def forward(samples, w_first, b_first, w_second, b_second, w_third):
    first = jax.nn.gelu(jnp.dot(samples.astype(jnp.float32), w_first.astype(jnp.float32), preferred_element_type=jnp.float32) * IN ** (-0.5) + b_first.astype(jnp.float32), approximate=True).astype(jnp.bfloat16)
    second = jax.nn.gelu(jnp.dot(first.astype(jnp.float32), w_second.astype(jnp.float32), preferred_element_type=jnp.float32) * H ** (-0.5) + b_second.astype(jnp.float32), approximate=True).astype(jnp.bfloat16)
    return jnp.dot(second.astype(jnp.float32), w_third.astype(jnp.float32), preferred_element_type=jnp.float32) * H ** (-0.5)

def solve_gain(amat, bmat):
    count = amat.shape[0]
    system = amat + count * jnp.eye(count, dtype=jnp.float32)
    factor = jnp.linalg.cholesky(system)
    middle = lax.linalg.triangular_solve(factor, bmat, left_side=True, lower=True, transpose_a=False)
    return lax.linalg.triangular_solve(factor, middle, left_side=True, lower=True, transpose_a=True)

def blend(theta, gain_low):
    count = theta.shape[0]
    per = theta.size // count
    width = math.gcd(per, 4096)
    blocks = theta.reshape(count, per // width, width).transpose(1, 0, 2)
    gain_tr = gain_low.T

    def mixone(block):
        full = block.astype(jnp.float32)
        center = (full - lax.optimization_barrier(jnp.mean(full, axis=0, keepdims=True))).astype(jnp.bfloat16)
        return jnp.dot(gain_tr.astype(jnp.float32), center.astype(jnp.float32), preferred_element_type=jnp.float32).astype(jnp.bfloat16)
    mixed = lax.map(mixone, blocks)
    return mixed.transpose(1, 0, 2).reshape(theta.shape)

def reference(samples, w_first, b_first, w_second, b_second, w_third, observed, perturb, variance):
    pred = lax.map(lambda p: forward(samples, p[0], p[1], p[2], p[3], p[4]), (w_first, b_first, w_second, b_second, w_third))
    resid = observed[None] + jnp.sqrt(variance)[None] * perturb - pred
    count = pred.shape[0]
    flatpred = pred.reshape(count, -1)
    flatres = resid.reshape(count, -1)
    devpred = flatpred - lax.optimization_barrier(jnp.mean(flatpred, axis=0, keepdims=True))
    scaled = devpred / variance.reshape(1, -1)
    amat = jnp.dot(scaled, devpred.T, precision=lax.Precision.HIGHEST)
    bmat = jnp.dot(scaled, flatres.T, precision=lax.Precision.HIGHEST)
    gain = solve_gain(amat, bmat)
    gain_low = gain.astype(jnp.bfloat16)
    return (blend(w_first, gain_low), blend(b_first, gain_low), blend(w_second, gain_low), blend(b_second, gain_low), blend(w_third, gain_low))
```

```python
import functools

import jax
import jax.numpy as jnp
from jax import lax
from jax.experimental import pallas as pl
from jax.experimental.pallas import tpu as pltpu
from jax.sharding import PartitionSpec as P

MESH = pl.DeviceIdType.MESH
ROWS = 16
LANES = 128


def holder(e):
    y, x = e // 8, lax.rem(e // 2, 4)
    return y * 32 + (lax.rem(x + y, 4) + 4 * lax.rem(e, 2)) * 4 + x


def own_tile(me):
    y, z, x = me // 32, lax.rem(me // 4, 8), lax.rem(me, 4)
    return lax.rem(z, 4) == lax.rem(x + y, 4), y * 8 + x * 2 + z // 4


BIAS_AT = 4


def exchange_kernel(
    members,
    gain_tr,
    w_first,
    w_second,
    w_third,
    bias,
    new_first,
    new_second,
    new_third,
    new_bias,
    slab,
    mixed,
    weights,
    spread,
    avg,
    send_sem,
    recv_sem,
    send_extra,
    recv_extra,
    back_send,
    back_extra,
    back_recv,
):
    me, core = lax.axis_index("member"), lax.axis_index("pair")
    y = pltpu.get_barrier_semaphore()
    wide = w_second.shape[1]
    narrow = w_first.shape[1] // 4
    main = wide + narrow
    holds, tile = own_tile(me)
    mine = pl.ds(pl.multiple_of(me * ROWS, ROWS), ROWS)

    def greet(i, _):
        peer = lax.rem(me + i, members)
        pl.semaphore_signal(y, inc=1, device_id=(peer, core), device_id_type=MESH)
        return 0

    lax.fori_loop(1, members, greet, 0)
    pl.semaphore_wait(y, members - 1)

    def rows_of(p):
        return pl.ds(pl.multiple_of(p * ROWS, ROWS), ROWS)

    def first_part(p):
        return (
            pl.ds(pl.multiple_of((p // 4) * ROWS, ROWS), ROWS),
            pl.ds(pl.multiple_of(lax.rem(p, 4) * narrow, narrow), narrow),
        )

    def third_part(e):
        return (
            pl.ds(pl.multiple_of((e // 8) * ROWS, ROWS), ROWS),
            pl.ds(pl.multiple_of(lax.rem(e, 8) * LANES, LANES), LANES),
        )

    def remote(src, dst, send, recv, peer):
        return pltpu.make_async_remote_copy(
            src_ref=src,
            dst_ref=dst,
            send_sem=send,
            recv_sem=recv,
            device_id=(peer, core),
            device_id_type=MESH,
        )

    cols_second, cols_first, cols_extra = pl.ds(0, wide), pl.ds(wide, narrow), pl.ds(main, LANES)

    def push(i, _):
        p = lax.rem(me + i, members)
        remote(w_second.at[rows_of(p), :], slab.at[mine, cols_second], send_sem, recv_sem, p).start()
        remote(w_first.at[first_part(p)], slab.at[mine, cols_first], send_sem, recv_sem, p).start()
        return 0

    lax.fori_loop(1, members, push, 0)
    pltpu.make_async_copy(w_second.at[mine, :], slab.at[mine, cols_second], recv_sem).start()
    pltpu.make_async_copy(w_first.at[first_part(me)], slab.at[mine, cols_first], recv_sem).start()

    def push_extra(e, _):
        p = holder(e)
        here = p == me

        @pl.when(here)
        def _():
            pltpu.make_async_copy(
                w_third.at[third_part(e)], slab.at[mine, cols_extra], recv_extra
            ).start()

        @pl.when(jnp.logical_not(here))
        def _():
            remote(
                w_third.at[third_part(e)], slab.at[mine, cols_extra], send_extra, recv_extra, p
            ).start()

        return 0

    lax.fori_loop(0, 32, push_extra, 0)

    @pl.when(me == BIAS_AT)
    def _():
        pltpu.make_async_copy(bias, slab.at[mine, cols_extra], recv_extra).start()

    @pl.when(me != BIAS_AT)
    def _():
        remote(bias, slab.at[mine, cols_extra], send_extra, recv_extra, BIAS_AT).start()

    extra_here = jnp.logical_or(holds, me == BIAS_AT)

    count = members * ROWS
    at = lax.broadcasted_iota(jnp.int32, (members, count), 1) // ROWS
    who = lax.broadcasted_iota(jnp.int32, (members, count), 0)
    spread[...] = jnp.where(at == who, 1.0, 0.0).astype(jnp.bfloat16)

    pltpu.make_async_copy(
        slab.at[:, pl.ds(0, main)], slab.at[:, pl.ds(0, main)], recv_sem
    ).wait()

    @pl.when(extra_here)
    def _():
        pltpu.make_async_copy(slab.at[:, cols_extra], slab.at[:, cols_extra], recv_extra).wait()

    group = weights.shape[0]
    peers = group // ROWS

    total = main + LANES
    tr = lax.broadcasted_iota(jnp.int32, (ROWS, count), 1) % ROWS
    tw = lax.broadcasted_iota(jnp.int32, (ROWS, count), 0)
    same = jnp.where(tr == tw, 1.0, 0.0).astype(jnp.bfloat16)

    @pl.loop(0, total // LANES)
    def _(n):
        c = pl.ds(pl.multiple_of(n * LANES, LANES), LANES)
        avg[:, c] = jnp.dot(same, slab[:, c], preferred_element_type=jnp.float32) * (1.0 / members)

    @pl.loop(0, members // peers)
    def _(g):
        jr = lax.broadcasted_iota(jnp.int32, (group, members), 0) // ROWS + g * peers
        jj = lax.broadcasted_iota(jnp.int32, (group, members), 1)
        pick = jnp.where(jr == jj, 1.0, 0.0).astype(jnp.bfloat16)
        rep = jnp.dot(pick, gain_tr[...], preferred_element_type=jnp.float32)
        weight_sum = jnp.sum(rep, axis=1, keepdims=True)
        rep16 = rep.astype(jnp.bfloat16)

        @pl.loop(0, count // 512)
        def _(q):
            c = pl.ds(pl.multiple_of(q * 512, 512), 512)
            full = jnp.dot(rep16, spread[:, c], preferred_element_type=jnp.float32)
            r0 = lax.broadcasted_iota(jnp.int32, (group, 512), 0) % ROWS
            r1 = lax.broadcasted_iota(jnp.int32, (group, 512), 1) % ROWS
            weights[:, c] = jnp.where(r0 == r1, full, 0.0).astype(jnp.bfloat16)

        out_rows = pl.ds(pl.multiple_of(g * group, group), group)

        def mix(c, width):
            acc = jnp.dot(weights[...], slab[:, c], preferred_element_type=jnp.float32)
            means = jnp.broadcast_to(avg[:, c][None], (peers, ROWS, width)).reshape(group, width)
            mixed[out_rows, c] = (acc - weight_sum * means).astype(jnp.bfloat16)

        @pl.loop(0, main // 256)
        def _(n):
            mix(pl.ds(pl.multiple_of(n * 256, 256), 256), 256)

        @pl.when(extra_here)
        def _():
            mix(cols_extra, LANES)

        def back(i, _):
            j = g * peers + i
            here = j == me

            @pl.when(here)
            def _():
                pltpu.make_async_copy(
                    mixed.at[mine, cols_second], new_second.at[mine, :], back_recv.at[0]
                ).start()
                pltpu.make_async_copy(
                    mixed.at[mine, cols_first], new_first.at[first_part(me)], back_recv.at[1]
                ).start()

                @pl.when(holds)
                def _():
                    pltpu.make_async_copy(
                        mixed.at[mine, cols_extra], new_third.at[third_part(tile)], back_recv.at[2]
                    ).start()

                @pl.when(me == BIAS_AT)
                def _():
                    pltpu.make_async_copy(
                        mixed.at[mine, cols_extra], new_bias, back_recv.at[3]
                    ).start()

            @pl.when(jnp.logical_not(here))
            def _():
                remote(
                    mixed.at[rows_of(j), cols_second], new_second.at[mine, :], back_send, back_recv.at[0], j
                ).start()
                remote(
                    mixed.at[rows_of(j), cols_first],
                    new_first.at[first_part(me)],
                    back_send,
                    back_recv.at[1],
                    j,
                ).start()

                @pl.when(holds)
                def _():
                    remote(
                        mixed.at[rows_of(j), cols_extra],
                        new_third.at[third_part(tile)],
                        back_extra,
                        back_recv.at[2],
                        j,
                    ).start()

                @pl.when(me == BIAS_AT)
                def _():
                    remote(
                        mixed.at[rows_of(j), cols_extra], new_bias, back_extra, back_recv.at[3], j
                    ).start()

            return 0

        lax.fori_loop(0, peers, back, 0)

    def drain(ref, sem):
        pltpu.make_async_copy(ref, ref, sem).wait()

    others = pl.ds(0, (members - 1) * ROWS)
    drain(slab.at[others, pl.ds(0, main)], send_sem)
    at_most = 33 * ROWS

    @pl.when(extra_here)
    def _():
        drain(slab.at[pl.ds(0, at_most - ROWS), cols_extra], send_extra)
        drain(slab.at[others, cols_extra], back_extra)

    @pl.when(jnp.logical_not(extra_here))
    def _():
        drain(slab.at[pl.ds(0, at_most), cols_extra], send_extra)

    drain(new_second, back_recv.at[0])
    drain(new_first, back_recv.at[1])
    drain(new_third, back_recv.at[2])
    drain(new_bias, back_recv.at[3])
    drain(mixed.at[others, pl.ds(0, main)], back_send)


def exchange(gain_tr, w_first, w_second, w_third, bias, members):
    anywhere = pl.BlockSpec(memory_space=pl.ANY)
    wide = w_second.shape[1] + w_first.shape[1] // 4 + LANES
    count = members * ROWS
    dma = pltpu.SemaphoreType.DMA
    return pl.pallas_call(
        functools.partial(exchange_kernel, members),
        out_shape=[jax.ShapeDtypeStruct(a.shape, a.dtype) for a in (w_first, w_second, w_third, bias)],
        in_specs=[pl.BlockSpec(memory_space=pltpu.VMEM)] + [anywhere] * 4,
        out_specs=[anywhere] * 4,
        scratch_shapes=[
            pltpu.VMEM((count, wide), jnp.bfloat16),
            pltpu.VMEM((count, wide), jnp.bfloat16),
            pltpu.VMEM((512, count), jnp.bfloat16),
            pltpu.VMEM((members, count), jnp.bfloat16),
            pltpu.VMEM((ROWS, wide), jnp.float32),
            dma,
            dma,
            dma,
            dma,
            dma,
            dma,
            dma((4,)),
        ],
        compiler_params=pltpu.CompilerParams(
            collective_id=0, has_side_effects=True, vmem_limit_bytes=50 << 20
        ),
    )(gain_tr, w_first, w_second, w_third, bias)


def solve_gain(amat, bmat):
    count = amat.shape[0]
    system = amat + count * jnp.eye(count, dtype=jnp.float32)
    factor = jnp.linalg.cholesky(system)
    middle = lax.linalg.triangular_solve(
        factor, bmat, left_side=True, lower=True, transpose_a=False
    )
    return lax.linalg.triangular_solve(factor, middle, left_side=True, lower=True, transpose_a=True)


def moments(allpred, allres, var_cols):
    devpred = allpred - jnp.mean(allpred, axis=0, keepdims=True)
    scaled = devpred / var_cols
    amat = jnp.dot(scaled, devpred.T, precision=lax.Precision.HIGHEST)
    bmat = jnp.dot(scaled, allres.T, precision=lax.Precision.HIGHEST)
    return (amat, bmat)


def body(samples, w_first, b_first, w_second, b_second, w_third, observed, perturb, variance):
    in_scale = samples.shape[1] ** (-0.5)
    hid_scale = w_second.shape[1] ** (-0.5)
    first = jax.nn.gelu(
        jnp.dot(samples, w_first[0], preferred_element_type=jnp.float32) * in_scale
        + b_first[0].astype(jnp.float32),
        approximate=True,
    ).astype(jnp.bfloat16)
    second_w = w_second[0]
    summed = jnp.dot(
        lax.all_gather(first, "pair", axis=1, tiled=True),
        second_w,
        preferred_element_type=jnp.float32,
    )
    second = jax.nn.gelu(
        summed * hid_scale + b_second[0].astype(jnp.float32), approximate=True
    ).astype(jnp.bfloat16)
    partial_out = jnp.dot(second, w_third[0], preferred_element_type=jnp.float32) * hid_scale
    pred = lax.psum(partial_out, "pair")
    resid = observed + jnp.sqrt(variance) * perturb[0] - pred
    half = pred.shape[0] // 2
    row_start = lax.axis_index("pair") * half
    pred_half = lax.dynamic_slice_in_dim(pred, row_start, half, 0).reshape(1, -1)
    res_half = lax.dynamic_slice_in_dim(resid, row_start, half, 0).reshape(1, -1)
    var_half = lax.dynamic_slice_in_dim(variance, row_start, half, 0).reshape(1, -1)
    allpred, allres = (
        lax.all_gather(pred_half, "member", axis=0, tiled=True),
        lax.all_gather(res_half, "member", axis=0, tiled=True),
    )
    amat, bmat = moments(allpred, allres, var_half)
    amat, bmat = lax.psum((amat, bmat), "pair")
    gain = solve_gain(amat, bmat)
    gain_tr = gain.astype(jnp.bfloat16).T
    members = lax.axis_size("member")
    bias = jnp.concatenate([b_first.reshape(8, -1), b_second.reshape(8, -1)], axis=0)
    new_first, new_second, new_third, new_bias = exchange(
        gain_tr, w_first[0], w_second[0], w_third[0].T, bias, members
    )
    return (
        new_first[None],
        new_bias[:8].reshape(b_first.shape),
        new_second[None],
        new_bias[8:].reshape(b_second.shape),
        new_third.T[None],
    )


def solution(mesh):
    in_specs = (
        P(),
        P("member", None, "pair"),
        P("member", "pair"),
        P("member", None, "pair"),
        P("member", "pair"),
        P("member", "pair", None),
        P(),
        P("member", None, None),
        P(),
    )
    out_specs = (
        P("member", None, "pair"),
        P("member", "pair"),
        P("member", None, "pair"),
        P("member", "pair"),
        P("member", "pair", None),
    )
    return jax.shard_map(body, mesh=mesh, in_specs=in_specs, out_specs=out_specs, check_vma=False)
```

```python
import functools

import jax
import jax.numpy as jnp
from jax import lax
from jax.experimental import pallas as pl
from jax.experimental.pallas import tpu as pltpu
from jax.sharding import PartitionSpec as P

MESH = pl.DeviceIdType.MESH
ROWS = 16
LANES = 128
THIRDS = 32
BIAS_AT = 4
PACE = 8
WINDOW = 4
GROUP = 512
LAST = (((1,), (1,)), ((), ()))


def peer_at(me, i):
    y, z, x = me // 32, lax.rem(me // 4, 8), lax.rem(me, 4)
    dz, dx, dy = i & 7, (i >> 3) & 3, i >> 5
    return ((y + dy) & 3) * 32 + ((z + dz) & 7) * 4 + ((x + dx) & 3)


def holder(e):
    y, x = e // 8, lax.rem(e // 2, 4)
    return y * 32 + (lax.rem(x + y, 4) + 4 * lax.rem(e, 2)) * 4 + x


def own_tile(me):
    y, z, x = me // 32, lax.rem(me // 4, 8), lax.rem(me, 4)
    return lax.rem(z, 4) == lax.rem(x + y, 4), y * 8 + x * 2 + z // 4


def kernel(
    members,
    in_scale,
    hid_scale,
    samples,
    w_first,
    b_first,
    w_second,
    b_second,
    w_third_hbm,
    observed,
    perturb,
    variance,
    new_first,
    new_bfirst,
    new_second,
    new_bsecond,
    new_third,
    slab,
    mixed,
    weights,
    spread,
    avg,
    inputs,
    first_w,
    second_w,
    third_w,
    act_own,
    act_peer,
    second,
    out_t,
    out_peer,
    outgoing,
    columns,
    moments,
    partials,
    row,
    row_peer,
    system,
    spare_a,
    spare_b,
    spare_c,
    bias_wide,
    bias,
    bias_back,
    load_sem,
    send_sem,
    recv_sem,
    send_extra,
    recv_extra,
    pair_send,
    pair_recv,
    small_send,
    small_recv,
    back_send,
    back_extra,
    back_recv,
):
    me, core = lax.axis_index("member"), lax.axis_index("pair")
    other = 1 - core
    spares = (spare_a, spare_b, spare_c)
    wide = w_second.shape[1]
    narrow = w_first.shape[1] // 4
    main = wide + narrow
    count = members * ROWS
    holds, tile = own_tile(me)
    extra_here = jnp.logical_or(holds, me == BIAS_AT)

    def rows_of(p):
        return pl.ds(pl.multiple_of(p * ROWS, ROWS), ROWS)

    def first_part(p):
        return (
            pl.ds(pl.multiple_of((p // 4) * ROWS, ROWS), ROWS),
            pl.ds(pl.multiple_of(lax.rem(p, 4) * narrow, narrow), narrow),
        )

    def third_part(e):
        return (
            pl.ds(pl.multiple_of((e // 8) * ROWS, ROWS), ROWS),
            pl.ds(pl.multiple_of(lax.rem(e, 8) * LANES, LANES), LANES),
        )

    def remote(src, dst, send, recv, peer, to_core=None):
        return pltpu.make_async_remote_copy(
            src_ref=src,
            dst_ref=dst,
            send_sem=send,
            recv_sem=recv,
            device_id=(peer, core if to_core is None else to_core),
            device_id_type=MESH,
        )

    def drain(ref, sem):
        pltpu.make_async_copy(ref, ref, sem).wait()

    mine = rows_of(me)
    cols_second, cols_first, cols_extra = pl.ds(0, wide), pl.ds(wide, narrow), pl.ds(main, LANES)

    barrier = pltpu.get_barrier_semaphore()

    def greet(i, _):
        pl.semaphore_signal(
            barrier, inc=1, device_id=(peer_at(me, i), core), device_id_type=MESH
        )
        return 0

    lax.fori_loop(1, members, greet, 0)
    pl.semaphore_signal(barrier, inc=1, device_id=(me, other), device_id_type=MESH)

    loads = [
        pltpu.make_async_copy(samples, inputs, load_sem.at[0]),
        pltpu.make_async_copy(w_first, first_w, load_sem.at[1]),
        pltpu.make_async_copy(w_second, second_w, load_sem.at[2]),
        pltpu.make_async_copy(w_third_hbm, third_w, load_sem.at[3]),
    ]
    for load in loads:
        load.start()

    def bias_rows(i, ref, at):
        bias_wide[at + i : at + i + 1, :] = ref[:, i * LANES : (i + 1) * LANES].astype(jnp.float32)

    for i in range(8):
        bias_rows(i, b_first, 0)
        bias_rows(i, b_second, 8)
    bias[...] = bias_wide[...].astype(jnp.bfloat16)

    pl.semaphore_wait(barrier, members)

    def push(i, g):
        p = peer_at(me, i)
        remote(
            w_second.at[rows_of(p), :], slab.at[mine, cols_second], send_sem.at[g], recv_sem, p
        ).start()
        remote(
            w_first.at[first_part(p)], slab.at[mine, cols_first], send_sem.at[g], recv_sem, p
        ).start()

    def push_group(g):
        def one(i, _):
            push(i, g)
            return 0

        lax.fori_loop(max(1, g * PACE), (g + 1) * PACE, one, 0)

    def sent_group(g):
        n = (PACE if g else PACE - 1) * ROWS
        drain(slab.at[pl.ds(0, n), pl.ds(0, main)], send_sem.at[g])

    groups = members // PACE
    state = [0]

    def pump(n):
        for _ in range(n):
            g = state[0]
            if g >= groups:
                return
            if g >= WINDOW:
                sent_group(g - WINDOW)
            push_group(g)
            state[0] = g + 1

    def push_extra(e, _):
        p = holder(e)
        here = p == me

        @pl.when(here)
        def _():
            pltpu.make_async_copy(
                w_third_hbm.at[third_part(e)], slab.at[mine, cols_extra], recv_extra
            ).start()

        @pl.when(jnp.logical_not(here))
        def _():
            remote(
                w_third_hbm.at[third_part(e)], slab.at[mine, cols_extra], send_extra, recv_extra, p
            ).start()

        return 0

    pltpu.make_async_copy(w_second.at[mine, :], slab.at[mine, cols_second], recv_sem).start()
    pltpu.make_async_copy(w_first.at[first_part(me)], slab.at[mine, cols_first], recv_sem).start()
    pump(WINDOW)

    loads[0].wait()
    loads[1].wait()

    @pl.loop(0, wide // 256)
    def _(n):
        c = pl.ds(pl.multiple_of(n * 256, 256), 256)
        h = jnp.dot(inputs[...], first_w[:, c], preferred_element_type=jnp.float32) * in_scale
        h = h + b_first[:, c].astype(jnp.float32)
        act_own[:, c] = jax.nn.gelu(h, approximate=True).astype(jnp.bfloat16)

    to_pair = remote(act_own, act_peer, pair_send.at[0], pair_recv.at[0], me, other)
    to_pair.start()
    pump(1)
    loads[2].wait()
    loads[3].wait()
    to_pair.wait()
    half = second_w.shape[0] // 2
    own_rows = pl.ds(pl.multiple_of(core * half, half), half)
    peer_rows = pl.ds(pl.multiple_of(other * half, half), half)

    @pl.loop(0, wide // 256)
    def _(n):
        c = pl.ds(pl.multiple_of(n * 256, 256), 256)
        h = jnp.dot(act_own[...], second_w[own_rows, c], preferred_element_type=jnp.float32)
        h = h + jnp.dot(act_peer[...], second_w[peer_rows, c], preferred_element_type=jnp.float32)
        h = h * hid_scale + b_second[:, c].astype(jnp.float32)
        second[:, c] = jax.nn.gelu(h, approximate=True).astype(jnp.bfloat16)

    out_t[...] = (
        lax.dot_general(third_w[...], second[...], LAST, preferred_element_type=jnp.float32)
        * hid_scale
    )
    part = out_t.shape[1] // 2
    own_cols = pl.ds(pl.multiple_of(core * part, part), part)
    peer_cols = pl.ds(pl.multiple_of(other * part, part), part)
    to_pair = remote(out_t.at[:, peer_cols], out_peer, pair_send.at[1], pair_recv.at[1], me, other)
    to_pair.start()
    pump(1)
    to_pair.wait()
    pred = out_t[:, own_cols] + out_peer[...]
    resid = observed[:, own_cols] + jnp.sqrt(variance[:, own_cols]) * perturb[:, own_cols] - pred
    tall = pred.shape[0]
    for k in range(2):
        outgoing[k * tall : (k + 1) * tall, 0:LANES] = pred[:, k * LANES : (k + 1) * LANES]
        outgoing[k * tall : (k + 1) * tall, LANES:] = resid[:, k * LANES : (k + 1) * LANES]

    def line(ref, p):
        return ref.at[pl.ds(p, 1), :]

    def scatter_rows(src, dst, k, whole):
        def one(i, _):
            p = peer_at(me, i)
            remote(
                src if whole else line(src, p), line(dst, me), small_send.at[k], small_recv.at[k], p
            ).start()
            return 0

        lax.fori_loop(1, members, one, 0)
        own = src if whole else line(src, me)
        pltpu.make_async_copy(own, line(dst, me), small_recv.at[k]).start()
        pltpu.make_async_copy(own, spares[k], small_send.at[k]).start()

    scatter_rows(outgoing, columns, 0, False)
    pump(1)
    drain(columns, small_recv.at[0])
    pred_all, res_all = columns[:, 0:LANES], columns[:, LANES:]
    dev = pred_all - jnp.mean(pred_all, axis=0, keepdims=True)
    var_at = core * part + (me // tall) * LANES
    var_rows = variance[:, pl.ds(pl.multiple_of(var_at, LANES), LANES)]
    its_row = lax.broadcasted_iota(jnp.int32, (tall, LANES), 0) == lax.rem(me, tall)
    var_here = jnp.sum(jnp.where(its_row, var_rows, 0.0), axis=0, keepdims=True)
    scaled = dev / var_here
    exact = lax.Precision.HIGHEST
    moments[:, 0:LANES] = lax.dot_general(
        scaled, dev, LAST, precision=exact, preferred_element_type=jnp.float32
    )
    moments[:, LANES:] = lax.dot_general(
        scaled, res_all, LAST, precision=exact, preferred_element_type=jnp.float32
    )

    scatter_rows(moments, partials, 1, False)
    pump(1)
    drain(partials, small_recv.at[1])
    row[...] = jnp.sum(partials[...], axis=0, keepdims=True)
    to_pair = remote(row, row_peer, pair_send.at[2], pair_recv.at[2], me, other)
    to_pair.start()
    to_pair.wait()
    row[...] = row[...] + row_peer[...]
    scatter_rows(row, system, 2, True)
    pump(1)
    lax.fori_loop(0, THIRDS, push_extra, 0)

    @pl.when(me == BIAS_AT)
    def _():
        pltpu.make_async_copy(bias, slab.at[mine, cols_extra], recv_extra).start()

    @pl.when(me != BIAS_AT)
    def _():
        remote(bias, slab.at[mine, cols_extra], send_extra, recv_extra, BIAS_AT).start()

    at = lax.broadcasted_iota(jnp.int32, (members, count), 1) // ROWS
    who = lax.broadcasted_iota(jnp.int32, (members, count), 0)
    spread[...] = jnp.where(at == who, 1.0, 0.0).astype(jnp.bfloat16)
    drain(system, small_recv.at[2])

    d0 = lax.broadcasted_iota(jnp.int32, (members, members), 0)
    d1 = lax.broadcasted_iota(jnp.int32, (members, members), 1)
    system[:, 0:members] = system[:, 0:members] + jnp.where(d0 == d1, float(members), 0.0)
    lane = lax.broadcasted_iota(jnp.int32, (1, 2 * members), 1)

    def eliminate(i, _):
        now = system[...]
        top = system[pl.ds(i, 1), :]
        col = jnp.sum(jnp.where(lane == i, now, 0.0), axis=1, keepdims=True)
        pivot = jnp.sum(jnp.where(lane == i, top, 0.0), axis=1, keepdims=True)
        top = top / pivot
        system[...] = now - col * top
        system[pl.ds(i, 1), :] = top
        return 0

    for k in range(8):
        step = members // 8
        lax.fori_loop(k * step, (k + 1) * step, eliminate, 0)
        pump(1)
    pump(groups)
    gain = system[:, members:].astype(jnp.bfloat16)
    spread_gain = gain

    peers = GROUP // ROWS

    def weigh(g):
        ir = lax.broadcasted_iota(jnp.int32, (GROUP, members), 0) // ROWS + g * peers
        jj = lax.broadcasted_iota(jnp.int32, (GROUP, members), 1)
        pick = jnp.where(peer_at(me, ir) == jj, 1.0, 0.0).astype(jnp.bfloat16)
        rep = lax.dot_general(pick, spread_gain, LAST, preferred_element_type=jnp.float32)
        rep16 = rep.astype(jnp.bfloat16)

        @pl.loop(0, count // 512)
        def _(q):
            c = pl.ds(pl.multiple_of(q * 512, 512), 512)
            full = jnp.dot(rep16, spread[:, c], preferred_element_type=jnp.float32)
            r0 = lax.broadcasted_iota(jnp.int32, (GROUP, 512), 0) % ROWS
            r1 = lax.broadcasted_iota(jnp.int32, (GROUP, 512), 1) % ROWS
            weights[pl.ds(0, GROUP), c] = jnp.where(r0 == r1, full, 0.0).astype(jnp.bfloat16)

        return jnp.sum(rep, axis=1, keepdims=True)

    tr = lax.broadcasted_iota(jnp.int32, (ROWS, count), 1) % ROWS
    tw = lax.broadcasted_iota(jnp.int32, (ROWS, count), 0)
    weights[pl.ds(GROUP, ROWS), :] = jnp.where(tr == tw, 1.0, 0.0).astype(jnp.bfloat16)

    def mix(g, weight_sum, c, width):
        out_rows = pl.ds(pl.multiple_of(g * GROUP, GROUP), GROUP)
        if isinstance(g, int):
            acc = jnp.dot(weights[...], slab[:, c], preferred_element_type=jnp.float32)
            avg[:, c] = acc[GROUP:, :] * (1.0 / members)
            acc = acc[:GROUP, :]
        else:
            acc = jnp.dot(
                weights[pl.ds(0, GROUP), :], slab[:, c], preferred_element_type=jnp.float32
            )
        means = jnp.broadcast_to(avg[:, c][None], (peers, ROWS, width)).reshape(GROUP, width)
        mixed[out_rows, c] = (acc - weight_sum * means).astype(jnp.bfloat16)

    def mix_all(g, weight_sum):
        @pl.loop(0, main // 256)
        def _(n):
            mix(g, weight_sum, pl.ds(pl.multiple_of(n * 256, 256), 256), 256)

        @pl.when(extra_here)
        def _():
            mix(g, weight_sum, cols_extra, LANES)

    def send_back(i, _):
        j = peer_at(me, i)
        remote(
            mixed.at[rows_of(i), cols_second], new_second.at[mine, :], back_send, back_recv.at[0], j
        ).start()
        remote(
            mixed.at[rows_of(i), cols_first],
            new_first.at[first_part(me)],
            back_send,
            back_recv.at[1],
            j,
        ).start()

        @pl.when(holds)
        def _():
            remote(
                mixed.at[rows_of(i), cols_extra],
                new_third.at[third_part(tile)],
                back_extra,
                back_recv.at[2],
                j,
            ).start()

        @pl.when(me == BIAS_AT)
        def _():
            remote(
                mixed.at[rows_of(i), cols_extra], bias_back, back_extra, back_recv.at[3], j
            ).start()

        return 0

    def keep_own():
        here = pl.ds(0, ROWS)
        pltpu.make_async_copy(
            mixed.at[here, cols_second], new_second.at[mine, :], back_recv.at[0]
        ).start()
        pltpu.make_async_copy(
            mixed.at[here, cols_first], new_first.at[first_part(me)], back_recv.at[1]
        ).start()

        @pl.when(holds)
        def _():
            pltpu.make_async_copy(
                mixed.at[here, cols_extra], new_third.at[third_part(tile)], back_recv.at[2]
            ).start()

        @pl.when(me == BIAS_AT)
        def _():
            pltpu.make_async_copy(mixed.at[here, cols_extra], bias_back, back_recv.at[3]).start()

    weight_sum = weigh(0)
    drain(slab.at[:, pl.ds(0, main)], recv_sem)

    @pl.when(extra_here)
    def _():
        drain(slab.at[:, cols_extra], recv_extra)

    mix_all(0, weight_sum)
    keep_own()
    lax.fori_loop(1, peers, send_back, 0)

    @pl.loop(1, members // peers)
    def _(g):
        mix_all(g, weigh(g))
        lax.fori_loop(g * peers, (g + 1) * peers, send_back, 0)

    others = pl.ds(0, (members - 1) * ROWS)
    for g in range(groups - WINDOW, groups):
        sent_group(g)
    for k in range(3):
        drain(outgoing, small_send.at[k])

    @pl.when(extra_here)
    def _():
        drain(slab.at[pl.ds(0, THIRDS * ROWS), cols_extra], send_extra)
        drain(slab.at[others, cols_extra], back_extra)

    @pl.when(jnp.logical_not(extra_here))
    def _():
        drain(slab.at[pl.ds(0, (THIRDS + 1) * ROWS), cols_extra], send_extra)

    drain(bias_back, back_recv.at[3])
    bias_wide[...] = bias_back[...].astype(jnp.float32)
    for i in range(8):
        c = slice(i * LANES, (i + 1) * LANES)
        new_bfirst[:, c] = bias_wide[i : i + 1, :].astype(jnp.bfloat16)
        new_bsecond[:, c] = bias_wide[8 + i : 9 + i, :].astype(jnp.bfloat16)
    drain(new_first, back_recv.at[1])
    drain(new_third, back_recv.at[2])
    drain(new_second, back_recv.at[0])
    drain(mixed.at[others, pl.ds(0, main)], back_send)


def body(samples, w_first, b_first, w_second, b_second, w_third, observed, perturb, variance):
    members = lax.axis_size("member")
    in_scale = samples.shape[1] ** (-0.5)
    hid_scale = w_second.shape[1] ** (-0.5)
    first_w, second_w, third_w = w_first[0], w_second[0], w_third[0].T
    count = members * ROWS
    wide = second_w.shape[1] + first_w.shape[1] // 4 + LANES
    batch, hidden, outs = samples.shape[0], second_w.shape[1], third_w.shape[0]
    anywhere = pl.BlockSpec(memory_space=pl.ANY)
    onchip = pl.BlockSpec(memory_space=pltpu.VMEM)
    dma = pltpu.SemaphoreType.DMA
    low, full = jnp.bfloat16, jnp.float32
    shapes = (first_w, b_first, second_w, b_second, third_w)
    new_first, new_bfirst, new_second, new_bsecond, new_third = pl.pallas_call(
        functools.partial(kernel, members, in_scale, hid_scale),
        out_shape=[jax.ShapeDtypeStruct(a.shape, a.dtype) for a in shapes],
        in_specs=[anywhere, anywhere, onchip, anywhere, onchip, anywhere, onchip, onchip, onchip],
        out_specs=[anywhere, onchip, anywhere, onchip, anywhere],
        scratch_shapes=[
            pltpu.VMEM((count, wide), low),
            pltpu.VMEM((count, wide), low),
            pltpu.VMEM((GROUP + ROWS, count), low),
            pltpu.VMEM((members, count), low),
            pltpu.VMEM((ROWS, wide), full),
            pltpu.VMEM(samples.shape, low),
            pltpu.VMEM(first_w.shape, low),
            pltpu.VMEM(second_w.shape, low),
            pltpu.VMEM(third_w.shape, low),
            pltpu.VMEM((batch, hidden), low),
            pltpu.VMEM((batch, hidden), low),
            pltpu.VMEM((batch, hidden), low),
            pltpu.VMEM((outs, batch), full),
            pltpu.VMEM((outs, batch // 2), full),
            pltpu.VMEM((members, 2 * LANES), full),
            pltpu.VMEM((members, 2 * LANES), full),
            pltpu.VMEM((members, 2 * LANES), full),
            pltpu.VMEM((members, 2 * LANES), full),
            pltpu.VMEM((1, 2 * LANES), full),
            pltpu.VMEM((1, 2 * LANES), full),
            pltpu.VMEM((members, 2 * LANES), full),
            pltpu.VMEM((1, 2 * LANES), full),
            pltpu.VMEM((1, 2 * LANES), full),
            pltpu.VMEM((1, 2 * LANES), full),
            pltpu.VMEM((ROWS, LANES), full),
            pltpu.VMEM((ROWS, LANES), low),
            pltpu.VMEM((ROWS, LANES), low),
            dma((4,)),
            dma((members // PACE,)),
            dma,
            dma,
            dma,
            dma((3,)),
            dma((3,)),
            dma((3,)),
            dma((3,)),
            dma,
            dma,
            dma((4,)),
        ],
        compiler_params=pltpu.CompilerParams(
            collective_id=0, has_side_effects=True, vmem_limit_bytes=50 << 20
        ),
    )(
        samples,
        first_w,
        b_first,
        second_w,
        b_second,
        third_w,
        observed.T,
        perturb[0].T,
        variance.T,
    )
    return (new_first[None], new_bfirst, new_second[None], new_bsecond, new_third.T[None])


def solution(mesh):
    in_specs = (
        P(),
        P("member", None, "pair"),
        P("member", "pair"),
        P("member", None, "pair"),
        P("member", "pair"),
        P("member", "pair", None),
        P(),
        P("member", None, None),
        P(),
    )
    out_specs = (
        P("member", None, "pair"),
        P("member", "pair"),
        P("member", None, "pair"),
        P("member", "pair"),
        P("member", "pair", None),
    )
    return jax.shard_map(body, mesh=mesh, in_specs=in_specs, out_specs=out_specs, check_vma=False)
```

```python
import functools

import jax
import jax.numpy as jnp
from jax import lax
from jax.experimental import pallas as pl
from jax.experimental.pallas import tpu as pltpu
from jax.sharding import PartitionSpec as P

MESH = pl.DeviceIdType.MESH
ROWS = 16
LANES = 128
THIRDS = 32
BIAS_AT = 4
PACE = 8
PLAN = (6, 2, 0, 2, 2, 0)
GROUP = 256
LAST = (((1,), (1,)), ((), ()))


def peer_at(me, i):
    y, z, x = me // 32, lax.rem(me // 4, 8), lax.rem(me, 4)
    dz, dx, dy = i & 7, (i >> 3) & 3, i >> 5
    return ((y + dy) & 3) * 32 + ((z + dz) & 7) * 4 + ((x + dx) & 3)


def holder(e):
    y, x = e // 8, lax.rem(e // 2, 4)
    return y * 32 + (lax.rem(x + y, 4) + 4 * lax.rem(e, 2)) * 4 + x


def own_tile(me):
    y, z, x = me // 32, lax.rem(me // 4, 8), lax.rem(me, 4)
    return lax.rem(z, 4) == lax.rem(x + y, 4), y * 8 + x * 2 + z // 4


def kernel(
    members,
    in_scale,
    hid_scale,
    samples,
    w_first,
    b_first_hbm,
    w_second,
    b_second_hbm,
    w_third_hbm,
    observed_hbm,
    perturb_hbm,
    variance_hbm,
    new_first,
    new_bfirst,
    new_second,
    new_bsecond,
    new_third,
    slab,
    mixed,
    weights,
    weight_sums,
    spread,
    avg,
    inputs,
    first_w,
    second_w,
    third_w,
    b_first,
    b_second,
    observed,
    perturb,
    variance,
    act_own,
    act_peer,
    second,
    out_t,
    out_peer,
    outgoing,
    columns,
    moments,
    partials,
    row,
    row_peer,
    system,
    spare_a,
    spare_b,
    spare_c,
    bias_wide,
    bias,
    bias_back,
    load_sem,
    send_sem,
    recv_sem,
    send_extra,
    recv_extra,
    pair_send,
    pair_recv,
    small_send,
    small_recv,
    back_send,
    back_recv,
):
    me, core = lax.axis_index("member"), lax.axis_index("pair")
    other = 1 - core
    spares = (spare_a, spare_b, spare_c)
    wide = w_second.shape[1]
    narrow = w_first.shape[1] // 4
    near = wide // 2
    main = wide + narrow
    count = members * ROWS
    holds, tile = own_tile(me)
    extra_here = jnp.logical_or(holds, me == BIAS_AT)

    def rows_of(p):
        return pl.ds(pl.multiple_of(p * ROWS, ROWS), ROWS)

    def first_part(p):
        return (
            pl.ds(pl.multiple_of((p // 4) * ROWS, ROWS), ROWS),
            pl.ds(pl.multiple_of(lax.rem(p, 4) * narrow, narrow), narrow),
        )

    def third_part(e):
        return (
            pl.ds(pl.multiple_of((e // 8) * ROWS, ROWS), ROWS),
            pl.ds(pl.multiple_of(lax.rem(e, 8) * LANES, LANES), LANES),
        )

    def remote(src, dst, send, recv, peer, to_core=None):
        return pltpu.make_async_remote_copy(
            src_ref=src,
            dst_ref=dst,
            send_sem=send,
            recv_sem=recv,
            device_id=(peer, core if to_core is None else to_core),
            device_id_type=MESH,
        )

    def drain(ref, sem):
        pltpu.make_async_copy(ref, ref, sem).wait()

    mine = rows_of(me)
    cols_near, cols_first = pl.ds(0, near), pl.ds(near, narrow)
    cols_far, cols_extra = pl.ds(near + narrow, near), pl.ds(main, LANES)
    cols_early = pl.ds(0, near + narrow)
    left_half, right_half = pl.ds(0, near), pl.ds(near, near)

    barrier = pltpu.get_barrier_semaphore()

    def greet(i, _):
        pl.semaphore_signal(
            barrier, inc=1, device_id=(peer_at(me, i), core), device_id_type=MESH
        )
        return 0

    lax.fori_loop(1, members, greet, 0)
    pl.semaphore_signal(barrier, inc=1, device_id=(me, other), device_id_type=MESH)

    part = samples.shape[0] // 2
    own_cols = pl.ds(pl.multiple_of(core * part, part), part)
    peer_cols = pl.ds(pl.multiple_of(other * part, part), part)
    arriving = (
        (samples, inputs),
        (w_first, first_w),
        (b_first_hbm, b_first),
        (b_second_hbm, b_second),
        (w_second, second_w),
        (w_third_hbm, third_w),
        (observed_hbm.at[:, own_cols], observed),
        (perturb_hbm.at[:, own_cols], perturb),
        (variance_hbm.at[:, own_cols], variance),
    )
    loads = [
        pltpu.make_async_copy(src, dst, load_sem.at[k]) for k, (src, dst) in enumerate(arriving)
    ]
    for load in loads:
        load.start()

    pl.semaphore_wait(barrier, members)

    groups = members // PACE
    units = 2 * groups
    issued = [0]

    def push_unit(u):
        g = u % groups

        def one(i, _):
            p = peer_at(me, i)
            if u < groups:
                remote(
                    w_second.at[rows_of(p), left_half],
                    slab.at[mine, cols_near],
                    send_sem.at[u],
                    recv_sem.at[0],
                    p,
                ).start()
                remote(
                    w_first.at[first_part(p)],
                    slab.at[mine, cols_first],
                    send_sem.at[u],
                    recv_sem.at[0],
                    p,
                ).start()
            else:
                remote(
                    w_second.at[rows_of(p), right_half],
                    slab.at[mine, cols_far],
                    send_sem.at[u],
                    recv_sem.at[1],
                    p,
                ).start()
            return 0

        lax.fori_loop(max(1, g * PACE), (g + 1) * PACE, one, 0)

    def sent_unit(u):
        n = (PACE if u % groups else PACE - 1) * ROWS
        drain(slab.at[pl.ds(0, n), cols_early if u < groups else cols_far], send_sem.at[u])

    def pump(n):
        for u in range(issued[0], min(units, issued[0] + n)):
            push_unit(u)
        issued[0] = min(units, issued[0] + n)

    def push_extra(e, _):
        p = holder(e)
        here = p == me

        @pl.when(here)
        def _():
            pltpu.make_async_copy(
                w_third_hbm.at[third_part(e)], slab.at[mine, cols_extra], recv_extra
            ).start()

        @pl.when(jnp.logical_not(here))
        def _():
            remote(
                w_third_hbm.at[third_part(e)], slab.at[mine, cols_extra], send_extra, recv_extra, p
            ).start()

        return 0

    pump(PLAN[0])
    here_first, here_near, here_far = (
        (w_first.at[first_part(me)], slab.at[mine, cols_first], recv_sem.at[0]),
        (w_second.at[mine, left_half], slab.at[mine, cols_near], recv_sem.at[0]),
        (w_second.at[mine, right_half], slab.at[mine, cols_far], recv_sem.at[1]),
    )
    for own in (here_first, here_near, here_far):
        pltpu.make_async_copy(*own).start()

    for load in loads[:3]:
        load.wait()

    @pl.loop(0, wide // 256)
    def _(n):
        c = pl.ds(pl.multiple_of(n * 256, 256), 256)
        h = jnp.dot(inputs[...], first_w[:, c], preferred_element_type=jnp.float32) * in_scale
        h = h + b_first[:, c].astype(jnp.float32)
        act_own[:, c] = jax.nn.gelu(h, approximate=True).astype(jnp.bfloat16)

    to_pair = remote(act_own, act_peer, pair_send.at[0], pair_recv.at[0], me, other)
    to_pair.start()
    pump(PLAN[1])
    for load in loads[3:]:
        load.wait()
    def bias_rows(i, ref, at):
        bias_wide[at + i : at + i + 1, :] = ref[:, i * LANES : (i + 1) * LANES].astype(jnp.float32)

    for i in range(8):
        bias_rows(i, b_first, 0)
        bias_rows(i, b_second, 8)
    bias[...] = bias_wide[...].astype(jnp.bfloat16)

    to_pair.wait()
    half = second_w.shape[0] // 2
    own_rows = pl.ds(pl.multiple_of(core * half, half), half)
    peer_rows = pl.ds(pl.multiple_of(other * half, half), half)

    @pl.loop(0, wide // 256)
    def _(n):
        c = pl.ds(pl.multiple_of(n * 256, 256), 256)
        h = jnp.dot(act_own[...], second_w[own_rows, c], preferred_element_type=jnp.float32)
        h = h + jnp.dot(act_peer[...], second_w[peer_rows, c], preferred_element_type=jnp.float32)
        h = h * hid_scale + b_second[:, c].astype(jnp.float32)
        second[:, c] = jax.nn.gelu(h, approximate=True).astype(jnp.bfloat16)

    out_t[...] = (
        lax.dot_general(third_w[...], second[...], LAST, preferred_element_type=jnp.float32)
        * hid_scale
    )
    to_pair = remote(out_t.at[:, peer_cols], out_peer, pair_send.at[1], pair_recv.at[1], me, other)
    to_pair.start()
    pump(PLAN[2])
    to_pair.wait()
    pred = out_t[:, own_cols] + out_peer[...]
    resid = observed[...] + jnp.sqrt(variance[...]) * perturb[...] - pred
    tall = pred.shape[0]
    for k in range(2):
        outgoing[k * tall : (k + 1) * tall, 0:LANES] = pred[:, k * LANES : (k + 1) * LANES]
        outgoing[k * tall : (k + 1) * tall, LANES:] = resid[:, k * LANES : (k + 1) * LANES]

    def line(ref, p):
        return ref.at[pl.ds(p, 1), :]

    def scatter_rows(src, dst, k, whole):
        def one(i, _):
            p = peer_at(me, i)
            remote(
                src if whole else line(src, p), line(dst, me), small_send.at[k], small_recv.at[k], p
            ).start()
            return 0

        lax.fori_loop(1, members, one, 0)
        own = src if whole else line(src, me)
        pltpu.make_async_copy(own, line(dst, me), small_recv.at[k]).start()
        pltpu.make_async_copy(own, spares[k], small_send.at[k]).start()

    scatter_rows(outgoing, columns, 0, False)
    pump(PLAN[3])
    drain(columns, small_recv.at[0])
    pred_all, res_all = columns[:, 0:LANES], columns[:, LANES:]
    dev = pred_all - jnp.mean(pred_all, axis=0, keepdims=True)
    var_at = (me // tall) * LANES
    var_rows = variance[:, pl.ds(pl.multiple_of(var_at, LANES), LANES)]
    its_row = lax.broadcasted_iota(jnp.int32, (tall, LANES), 0) == lax.rem(me, tall)
    var_here = jnp.sum(jnp.where(its_row, var_rows, 0.0), axis=0, keepdims=True)
    scaled = dev / var_here
    exact = lax.Precision.HIGHEST
    moments[:, 0:LANES] = lax.dot_general(
        scaled, dev, LAST, precision=exact, preferred_element_type=jnp.float32
    )
    moments[:, LANES:] = lax.dot_general(
        scaled, res_all, LAST, precision=exact, preferred_element_type=jnp.float32
    )

    scatter_rows(moments, partials, 1, False)
    pump(PLAN[4])
    drain(partials, small_recv.at[1])
    row[...] = jnp.sum(partials[...], axis=0, keepdims=True)
    to_pair = remote(row, row_peer, pair_send.at[2], pair_recv.at[2], me, other)
    to_pair.start()
    pump(PLAN[5])
    to_pair.wait()
    row[...] = row[...] + row_peer[...]
    scatter_rows(row, system, 2, True)
    lax.fori_loop(0, THIRDS, push_extra, 0)

    @pl.when(me == BIAS_AT)
    def _():
        pltpu.make_async_copy(bias, slab.at[mine, cols_extra], recv_extra).start()

    @pl.when(me != BIAS_AT)
    def _():
        remote(bias, slab.at[mine, cols_extra], send_extra, recv_extra, BIAS_AT).start()

    pump(units)

    at = lax.broadcasted_iota(jnp.int32, (members, count), 1) // ROWS
    who = lax.broadcasted_iota(jnp.int32, (members, count), 0)
    spread[...] = jnp.where(at == who, 1.0, 0.0).astype(jnp.bfloat16)
    drain(system, small_recv.at[2])

    d0 = lax.broadcasted_iota(jnp.int32, (members, members), 0)
    d1 = lax.broadcasted_iota(jnp.int32, (members, members), 1)
    system[:, 0:members] = system[:, 0:members] + jnp.where(d0 == d1, float(members), 0.0)
    lane = lax.broadcasted_iota(jnp.int32, (1, 2 * members), 1)

    def eliminate(i, _):
        now = system[...]
        top = system[pl.ds(i, 1), :]
        col = jnp.sum(jnp.where(lane == i, now, 0.0), axis=1, keepdims=True)
        pivot = jnp.sum(jnp.where(lane == i, top, 0.0), axis=1, keepdims=True)
        top = top / pivot
        system[...] = now - col * top
        system[pl.ds(i, 1), :] = top
        return 0

    lax.fori_loop(0, members, eliminate, 0)
    gain = system[:, members:].astype(jnp.bfloat16)
    peers = GROUP // ROWS

    @pl.loop(0, count // GROUP)
    def _(g):
        ir = lax.broadcasted_iota(jnp.int32, (GROUP, members), 0) // ROWS + g * peers
        jj = lax.broadcasted_iota(jnp.int32, (GROUP, members), 1)
        pick = jnp.where(peer_at(me, ir) == jj, 1.0, 0.0).astype(jnp.bfloat16)
        spread_out = lax.dot_general(pick, gain, LAST, preferred_element_type=jnp.float32)
        out_rows = pl.ds(pl.multiple_of(g * GROUP, GROUP), GROUP)
        weight_sums[out_rows, :] = jnp.sum(spread_out, axis=1, keepdims=True)
        spread_out = spread_out.astype(jnp.bfloat16)

        @pl.loop(0, count // 512)
        def _(q):
            c = pl.ds(pl.multiple_of(q * 512, 512), 512)
            full = jnp.dot(spread_out, spread[:, c], preferred_element_type=jnp.float32)
            r0 = lax.broadcasted_iota(jnp.int32, (GROUP, 512), 0) % ROWS
            r1 = lax.broadcasted_iota(jnp.int32, (GROUP, 512), 1) % ROWS
            weights[out_rows, c] = jnp.where(r0 == r1, full, 0.0).astype(jnp.bfloat16)

    tr = lax.broadcasted_iota(jnp.int32, (ROWS, count), 1) % ROWS
    tw = lax.broadcasted_iota(jnp.int32, (ROWS, count), 0)
    same = jnp.where(tr == tw, 1.0, 0.0).astype(jnp.bfloat16)

    def mean_of(c):
        avg[:, c] = jnp.dot(same, slab[:, c], preferred_element_type=jnp.float32) * (1.0 / members)

    def mix(g, c, width):
        out_rows = pl.ds(pl.multiple_of(g * GROUP, GROUP), GROUP)
        acc = jnp.dot(weights[out_rows, :], slab[:, c], preferred_element_type=jnp.float32)
        means = jnp.broadcast_to(avg[:, c][None], (peers, ROWS, width)).reshape(GROUP, width)
        mixed[out_rows, c] = (acc - weight_sums[out_rows, :] * means).astype(jnp.bfloat16)

    def tiles(lo, hi, do):
        @pl.loop(lo // 256, hi // 256)
        def _(n):
            do(pl.ds(pl.multiple_of(n * 256, 256), 256))

    targets = (
        (cols_near, new_second.at[mine, left_half]),
        (cols_first, new_first.at[first_part(me)]),
        (cols_far, new_second.at[mine, right_half]),
        (cols_extra, new_third.at[third_part(tile)]),
        (cols_extra, bias_back),
    )

    def send_back(i, k):
        c, dst = targets[k]
        send = back_send.at[k]
        remote(mixed.at[rows_of(i), c], dst, send, back_recv.at[k], peer_at(me, i)).start()

    def keep_own(k):
        c, dst = targets[k]
        pltpu.make_async_copy(mixed.at[pl.ds(0, ROWS), c], dst, back_recv.at[k]).start()

    def mix_and_send(early):
        def send(i):
            for k in (0, 1) if early else (2,):
                send_back(i, k)
            if not early:
                pl.when(holds)(lambda: send_back(i, 3))
                pl.when(me == BIAS_AT)(lambda: send_back(i, 4))

        @pl.loop(0, count // GROUP)
        def _(g):
            if early:
                tiles(0, near + narrow, lambda c: mix(g, c, 256))
            else:
                tiles(near + narrow, main, lambda c: mix(g, c, 256))
                pl.when(extra_here)(lambda: mix(g, cols_extra, LANES))

            @pl.loop(jnp.where(g == 0, 1, g * peers), (g + 1) * peers)
            def _(i):
                send(i)

        for k in (0, 1) if early else (2,):
            keep_own(k)
        if not early:
            pl.when(holds)(lambda: keep_own(3))
            pl.when(me == BIAS_AT)(lambda: keep_own(4))

    drain(slab.at[:, cols_early], recv_sem.at[0])
    tiles(0, near + narrow, mean_of)
    mix_and_send(True)
    drain(slab.at[:, cols_far], recv_sem.at[1])
    pl.when(extra_here)(lambda: drain(slab.at[:, cols_extra], recv_extra))
    tiles(near + narrow, main, mean_of)
    pl.when(extra_here)(lambda: mean_of(cols_extra))
    mix_and_send(False)

    others = pl.ds(0, (members - 1) * ROWS)
    for u in range(units):
        sent_unit(u)
    for k in range(3):
        drain(outgoing, small_send.at[k])

    @pl.when(extra_here)
    def _():
        drain(slab.at[pl.ds(0, THIRDS * ROWS), cols_extra], send_extra)

    @pl.when(jnp.logical_not(extra_here))
    def _():
        drain(slab.at[pl.ds(0, (THIRDS + 1) * ROWS), cols_extra], send_extra)

    for k in range(3):
        drain(mixed.at[others, targets[k][0]], back_send.at[k])
    pl.when(holds)(lambda: drain(mixed.at[others, cols_extra], back_send.at[3]))
    pl.when(me == BIAS_AT)(lambda: drain(mixed.at[others, cols_extra], back_send.at[4]))
    drain(new_second.at[:, left_half], back_recv.at[0])
    drain(new_first, back_recv.at[1])
    drain(bias_back, back_recv.at[4])
    bias_wide[...] = bias_back[...].astype(jnp.float32)
    for i in range(8):
        c = slice(i * LANES, (i + 1) * LANES)
        new_bfirst[:, c] = bias_wide[i : i + 1, :].astype(jnp.bfloat16)
        new_bsecond[:, c] = bias_wide[8 + i : 9 + i, :].astype(jnp.bfloat16)
    drain(new_third, back_recv.at[3])
    drain(new_second.at[:, right_half], back_recv.at[2])


def store_kernel(*refs):
    n = (len(refs) - 1) // 2
    sem = refs[-1]
    copies = []
    for src, dst in zip(refs[:n], refs[n : 2 * n]):
        cuts = max(1, src.shape[0] // 512)
        rows = src.shape[0] // cuts
        for k in range(cuts):
            at = pl.ds(k * rows, rows)
            copies.append(
                pltpu.make_async_copy(src.at[at, :], dst.at[at, :], sem.at[len(copies)])
            )
    for copy in copies:
        copy.start()
    for copy in copies:
        copy.wait()


def body(samples, w_first, b_first, w_second, b_second, w_third, observed, perturb, variance):
    members = lax.axis_size("member")
    in_scale = samples.shape[1] ** (-0.5)
    hid_scale = w_second.shape[1] ** (-0.5)
    first_w, second_w, third_w = w_first[0], w_second[0], w_third[0].T
    count = members * ROWS
    wide = second_w.shape[1] + first_w.shape[1] // 4 + LANES
    batch, hidden, outs = samples.shape[0], second_w.shape[1], third_w.shape[0]
    anywhere = pl.BlockSpec(memory_space=pl.ANY)
    onchip = pl.BlockSpec(memory_space=pltpu.VMEM)
    dma = pltpu.SemaphoreType.DMA
    low, full = jnp.bfloat16, jnp.float32
    shapes = (first_w, b_first, second_w, b_second, third_w)
    mixed = pl.pallas_call(
        functools.partial(kernel, members, in_scale, hid_scale),
        out_shape=[pltpu.VMEM(a.shape, a.dtype) for a in shapes],
        in_specs=[anywhere] * 9,
        out_specs=[onchip] * 5,
        scratch_shapes=[
            pltpu.VMEM((count, wide), low),
            pltpu.VMEM((count, wide), low),
            pltpu.VMEM((count, count), low),
            pltpu.VMEM((count, 1), full),
            pltpu.VMEM((members, count), low),
            pltpu.VMEM((ROWS, wide), full),
            pltpu.VMEM(samples.shape, low),
            pltpu.VMEM(first_w.shape, low),
            pltpu.VMEM(second_w.shape, low),
            pltpu.VMEM(third_w.shape, low),
            pltpu.VMEM(b_first.shape, low),
            pltpu.VMEM(b_second.shape, low),
            pltpu.VMEM((outs, batch // 2), full),
            pltpu.VMEM((outs, batch // 2), full),
            pltpu.VMEM((outs, batch // 2), full),
            pltpu.VMEM((batch, hidden), low),
            pltpu.VMEM((batch, hidden), low),
            pltpu.VMEM((batch, hidden), low),
            pltpu.VMEM((outs, batch), full),
            pltpu.VMEM((outs, batch // 2), full),
            pltpu.VMEM((members, 2 * LANES), full),
            pltpu.VMEM((members, 2 * LANES), full),
            pltpu.VMEM((members, 2 * LANES), full),
            pltpu.VMEM((members, 2 * LANES), full),
            pltpu.VMEM((1, 2 * LANES), full),
            pltpu.VMEM((1, 2 * LANES), full),
            pltpu.VMEM((members, 2 * LANES), full),
            pltpu.VMEM((1, 2 * LANES), full),
            pltpu.VMEM((1, 2 * LANES), full),
            pltpu.VMEM((1, 2 * LANES), full),
            pltpu.VMEM((ROWS, LANES), full),
            pltpu.VMEM((ROWS, LANES), low),
            pltpu.VMEM((ROWS, LANES), low),
            dma((9,)),
            dma((2 * members // PACE,)),
            dma((2,)),
            dma,
            dma,
            dma((3,)),
            dma((3,)),
            dma((3,)),
            dma((3,)),
            dma((5,)),
            dma((5,)),
        ],
        compiler_params=pltpu.CompilerParams(
            collective_id=0, has_side_effects=True, vmem_limit_bytes=50 << 20
        ),
    )(
        *(
            pltpu.with_memory_space_constraint(a, pltpu.HBM)
            for a in (
                samples,
                first_w,
                b_first,
                second_w,
                b_second,
                third_w,
                observed.T,
                perturb[0].T,
                variance.T,
            )
        )
    )
    new_first, new_bfirst, new_second, new_bsecond, new_third = pl.pallas_call(
        store_kernel,
        out_shape=[jax.ShapeDtypeStruct(a.shape, a.dtype) for a in shapes],
        in_specs=[anywhere] * 5,
        out_specs=[anywhere] * 5,
        scratch_shapes=[dma((8,))],
        compiler_params=pltpu.CompilerParams(vmem_limit_bytes=1 << 20),
    )(*(pltpu.with_memory_space_constraint(a, pltpu.VMEM) for a in mixed))
    return (new_first[None], new_bfirst, new_second[None], new_bsecond, new_third.T[None])


def solution(mesh):
    in_specs = (
        P(),
        P("member", None, "pair"),
        P("member", "pair"),
        P("member", None, "pair"),
        P("member", "pair"),
        P("member", "pair", None),
        P(),
        P("member", None, None),
        P(),
    )
    out_specs = (
        P("member", None, "pair"),
        P("member", "pair"),
        P("member", None, "pair"),
        P("member", "pair"),
        P("member", "pair", None),
    )
    return jax.shard_map(body, mesh=mesh, in_specs=in_specs, out_specs=out_specs, check_vma=False)
```

```python
import functools

import jax
import jax.numpy as jnp
from jax import lax
from jax.experimental import pallas as pl
from jax.experimental.pallas import tpu as pltpu
from jax.sharding import PartitionSpec as P

MESH = pl.DeviceIdType.MESH
ROWS = 16
LANES = 128
THIRDS = 32
BIAS_AT = 1
PACE = 8
PLAN = (6, 2, 0, 2, 0, 2, 2, 1, 2)
RING = 8
GROUP = 256
LAST = (((1,), (1,)), ((), ()))


def label(member):
    y, z, x = member // 32, (member >> 2) & 7, member & 3
    return y * 32 + x * 8 + z


def member_of(number):
    y, x, z = number >> 5, (number >> 3) & 3, number & 7
    return y * 32 + z * 4 + x


def peer_at(me, i):
    y, x, z = me >> 5, (me >> 3) & 3, me & 7
    dz, dx, dy = i & 7, (i >> 3) & 3, i >> 5
    return ((y + dy) & 3) * 32 + ((x + dx) & 3) * 8 + ((z + dz) & 7)


def holder(e):
    ring = e // 2
    return ring * 8 + (((ring >> 2) + ring) & 3) + 4 * (e & 1)


def own_tile(me):
    ring, z = me >> 3, me & 7
    return (z & 3) == (((ring >> 2) + ring) & 3), ring * 2 + (z >> 2)


def kernel(
    members,
    in_scale,
    hid_scale,
    samples,
    w_first,
    b_first_hbm,
    w_second,
    b_second_hbm,
    w_third_hbm,
    observed_hbm,
    perturb_hbm,
    variance_hbm,
    new_first,
    new_bfirst,
    new_second,
    new_bsecond,
    new_third,
    slab,
    mixed,
    weights,
    weight_sums,
    spread,
    avg,
    inputs,
    first_w,
    second_w,
    third_w,
    b_first,
    b_second,
    observed,
    perturb,
    variance,
    act_own,
    act_peer,
    second,
    out_t,
    out_peer,
    outgoing,
    columns,
    moments,
    partials,
    block,
    block_in,
    row,
    row_peer,
    block_out,
    blocks_out,
    system,
    spare_a,
    spare_b,
    spare_c,
    bias_wide,
    bias,
    bias_back,
    load_sem,
    send_sem,
    recv_sem,
    send_extra,
    recv_extra,
    pair_send,
    pair_recv,
    small_send,
    small_recv,
    back_send,
    back_recv,
):
    me, core = label(lax.axis_index("member")), lax.axis_index("pair")
    plane, spot = me >> 3, me & 7
    other = 1 - core
    wide = w_second.shape[1]
    narrow = w_first.shape[1] // 4
    near = wide // 2
    main = wide + narrow
    count = members * ROWS
    holds, tile = own_tile(me)
    extra_here = jnp.logical_or(holds, me == BIAS_AT)

    def rows_of(p):
        return pl.ds(pl.multiple_of(p * ROWS, ROWS), ROWS)

    def first_part(p):
        return (
            pl.ds(pl.multiple_of((p // 4) * ROWS, ROWS), ROWS),
            pl.ds(pl.multiple_of(lax.rem(p, 4) * narrow, narrow), narrow),
        )

    def third_part(e):
        return (
            pl.ds(pl.multiple_of((e // 8) * ROWS, ROWS), ROWS),
            pl.ds(pl.multiple_of(lax.rem(e, 8) * LANES, LANES), LANES),
        )

    def remote(src, dst, send, recv, peer, to_core=None):
        return pltpu.make_async_remote_copy(
            src_ref=src,
            dst_ref=dst,
            send_sem=send,
            recv_sem=recv,
            device_id=(member_of(peer), core if to_core is None else to_core),
            device_id_type=MESH,
        )

    def drain(ref, sem):
        pltpu.make_async_copy(ref, ref, sem).wait()

    mine = rows_of(me)
    cols_near, cols_first = pl.ds(0, near), pl.ds(near, narrow)
    cols_far, cols_extra = pl.ds(near + narrow, near), pl.ds(main, LANES)
    cols_early = pl.ds(0, near + narrow)
    left_half, right_half = pl.ds(0, near), pl.ds(near, near)

    barrier = pltpu.get_barrier_semaphore()

    def greet(i, _):
        pl.semaphore_signal(
            barrier,
            inc=1,
            device_id=(member_of(peer_at(me, i)), core),
            device_id_type=MESH,
        )
        return 0

    lax.fori_loop(1, members, greet, 0)
    pl.semaphore_signal(barrier, inc=1, device_id=(member_of(me), other), device_id_type=MESH)

    part = samples.shape[0] // 2
    own_cols = pl.ds(pl.multiple_of(core * part, part), part)
    peer_cols = pl.ds(pl.multiple_of(other * part, part), part)
    arriving = (
        (samples, inputs),
        (w_first, first_w),
        (b_first_hbm, b_first),
        (b_second_hbm, b_second),
        (w_second, second_w),
        (w_third_hbm, third_w),
        (observed_hbm.at[:, own_cols], observed),
        (perturb_hbm.at[:, own_cols], perturb),
        (variance_hbm.at[:, own_cols], variance),
    )
    loads = [
        pltpu.make_async_copy(src, dst, load_sem.at[k]) for k, (src, dst) in enumerate(arriving)
    ]
    for load in loads:
        load.start()

    pl.semaphore_wait(barrier, members)

    groups = members // PACE
    units = 2 * groups
    issued = [0]

    def push_unit(u):
        g = u % groups

        def one(i, _):
            p = peer_at(me, i)
            if u < groups:
                remote(
                    w_second.at[rows_of(p), left_half],
                    slab.at[mine, cols_near],
                    send_sem.at[u],
                    recv_sem.at[0],
                    p,
                ).start()
                remote(
                    w_first.at[first_part(p)],
                    slab.at[mine, cols_first],
                    send_sem.at[u],
                    recv_sem.at[0],
                    p,
                ).start()
            else:
                remote(
                    w_second.at[rows_of(p), right_half],
                    slab.at[mine, cols_far],
                    send_sem.at[u],
                    recv_sem.at[1],
                    p,
                ).start()
            return 0

        lax.fori_loop(max(1, g * PACE), (g + 1) * PACE, one, 0)

    def sent_unit(u):
        n = (PACE if u % groups else PACE - 1) * ROWS
        drain(slab.at[pl.ds(0, n), cols_early if u < groups else cols_far], send_sem.at[u])

    def pump(n):
        for u in range(issued[0], min(units, issued[0] + n)):
            push_unit(u)
        issued[0] = min(units, issued[0] + n)

    def push_extra(e, _):
        p = holder(e)
        here = p == me

        @pl.when(here)
        def _():
            pltpu.make_async_copy(
                w_third_hbm.at[third_part(e)], slab.at[mine, cols_extra], recv_extra
            ).start()

        @pl.when(jnp.logical_not(here))
        def _():
            remote(
                w_third_hbm.at[third_part(e)], slab.at[mine, cols_extra], send_extra, recv_extra, p
            ).start()

        return 0

    pump(PLAN[0])
    here_first, here_near, here_far = (
        (w_first.at[first_part(me)], slab.at[mine, cols_first], recv_sem.at[0]),
        (w_second.at[mine, left_half], slab.at[mine, cols_near], recv_sem.at[0]),
        (w_second.at[mine, right_half], slab.at[mine, cols_far], recv_sem.at[1]),
    )
    for own in (here_first, here_near, here_far):
        pltpu.make_async_copy(*own).start()

    for load in loads[:3]:
        load.wait()

    @pl.loop(0, wide // 256)
    def _(n):
        c = pl.ds(pl.multiple_of(n * 256, 256), 256)
        h = jnp.dot(inputs[...], first_w[:, c], preferred_element_type=jnp.float32) * in_scale
        h = h + b_first[:, c].astype(jnp.float32)
        act_own[:, c] = jax.nn.gelu(h, approximate=True).astype(jnp.bfloat16)

    to_pair = remote(act_own, act_peer, pair_send.at[0], pair_recv.at[0], me, other)
    to_pair.start()
    pump(PLAN[1])
    for load in loads[3:]:
        load.wait()
    def bias_rows(i, ref, at):
        bias_wide[at + i : at + i + 1, :] = ref[:, i * LANES : (i + 1) * LANES].astype(jnp.float32)

    for i in range(8):
        bias_rows(i, b_first, 0)
        bias_rows(i, b_second, 8)
    bias[...] = bias_wide[...].astype(jnp.bfloat16)

    to_pair.wait()
    half = second_w.shape[0] // 2
    own_rows = pl.ds(pl.multiple_of(core * half, half), half)
    peer_rows = pl.ds(pl.multiple_of(other * half, half), half)

    @pl.loop(0, wide // 256)
    def _(n):
        c = pl.ds(pl.multiple_of(n * 256, 256), 256)
        h = jnp.dot(act_own[...], second_w[own_rows, c], preferred_element_type=jnp.float32)
        h = h + jnp.dot(act_peer[...], second_w[peer_rows, c], preferred_element_type=jnp.float32)
        h = h * hid_scale + b_second[:, c].astype(jnp.float32)
        second[:, c] = jax.nn.gelu(h, approximate=True).astype(jnp.bfloat16)

    out_t[...] = (
        lax.dot_general(third_w[...], second[...], LAST, preferred_element_type=jnp.float32)
        * hid_scale
    )
    to_pair = remote(out_t.at[:, peer_cols], out_peer, pair_send.at[1], pair_recv.at[1], me, other)
    to_pair.start()
    pump(PLAN[2])
    to_pair.wait()
    pred = out_t[:, own_cols] + out_peer[...]
    resid = observed[...] + jnp.sqrt(variance[...]) * perturb[...] - pred
    tall = pred.shape[0]
    planes = members // RING
    for k in range(2):
        at, c = slice(k * tall, (k + 1) * tall), slice(k * LANES, (k + 1) * LANES)
        outgoing[at, 0:LANES] = pred[:, c]
        outgoing[at, LANES:] = resid[:, c]

    def over_planes(part_for, dst, k):
        def one(d, _):
            to = (plane + d) & (planes - 1)
            remote(
                part_for(to), dst.at[plane], small_send.at[k], small_recv.at[k], to * RING + spot
            ).start()
            return 0

        lax.fori_loop(1, planes, one, 0)
        pltpu.make_async_copy(part_for(plane), dst.at[plane], small_recv.at[k]).start()

    def over_ring(part_for, place, k):
        def one(d, _):
            to = (spot + d) & (RING - 1)
            remote(
                part_for(to), place, small_send.at[k], small_recv.at[k], plane * RING + to
            ).start()
            return 0

        lax.fori_loop(1, RING, one, 0)
        pltpu.make_async_copy(part_for(spot), place, small_recv.at[k]).start()

    def line(ref, p):
        return ref.at[pl.ds(p, 1), :]

    def scatter_row(i, _):
        p = peer_at(me, i)
        remote(line(outgoing, p), line(columns, me), small_send.at[0], small_recv.at[0], p).start()
        return 0

    lax.fori_loop(1, members, scatter_row, 0)
    pltpu.make_async_copy(line(outgoing, me), line(columns, me), small_recv.at[0]).start()
    pltpu.make_async_copy(line(outgoing, me), spare_c, small_send.at[0]).start()
    pump(PLAN[3])
    drain(columns, small_recv.at[0])
    pred_all, res_all = columns[:, 0:LANES], columns[:, LANES:]
    dev = pred_all - jnp.mean(pred_all, axis=0, keepdims=True)
    var_at = (me // tall) * LANES
    var_rows = variance[:, pl.ds(pl.multiple_of(var_at, LANES), LANES)]
    its_row = lax.broadcasted_iota(jnp.int32, (tall, LANES), 0) == lax.rem(me, tall)
    var_here = jnp.sum(jnp.where(its_row, var_rows, 0.0), axis=0, keepdims=True)
    scaled = dev / var_here
    exact = lax.Precision.HIGHEST
    for at, with_all in ((slice(0, LANES), dev), (slice(LANES, 2 * LANES), res_all)):
        sums = lax.dot_general(
            scaled, with_all, LAST, precision=exact, preferred_element_type=jnp.float32
        )
        moments[:, :, at] = sums.reshape(planes, RING, LANES)

    over_planes(lambda to: moments.at[to], partials, 2)
    pump(PLAN[5])
    drain(partials, small_recv.at[2])
    block[...] = jnp.sum(partials[...], axis=0)
    over_ring(lambda to: line(block, to), line(block_in, spot), 3)
    pltpu.make_async_copy(line(block, spot), spare_a, small_send.at[3]).start()
    pump(PLAN[6])
    drain(block_in, small_recv.at[3])
    row[...] = jnp.sum(block_in[...], axis=0, keepdims=True)
    to_pair = remote(row, row_peer, pair_send.at[2], pair_recv.at[2], me, other)
    to_pair.start()
    pump(PLAN[7])
    to_pair.wait()
    row[...] = row[...] + row_peer[...]
    over_ring(lambda to: row, line(block_out, spot), 4)
    pltpu.make_async_copy(row, spare_b, small_send.at[4]).start()
    pump(PLAN[8])
    drain(block_out, small_recv.at[4])
    over_planes(lambda to: block_out, blocks_out, 5)
    lax.fori_loop(0, THIRDS, push_extra, 0)

    @pl.when(me == BIAS_AT)
    def _():
        pltpu.make_async_copy(bias, slab.at[mine, cols_extra], recv_extra).start()

    @pl.when(me != BIAS_AT)
    def _():
        remote(bias, slab.at[mine, cols_extra], send_extra, recv_extra, BIAS_AT).start()

    pump(units)

    at = lax.broadcasted_iota(jnp.int32, (members, count), 1) // ROWS
    who = lax.broadcasted_iota(jnp.int32, (members, count), 0)
    spread[...] = jnp.where(at == who, 1.0, 0.0).astype(jnp.bfloat16)
    drain(blocks_out, small_recv.at[5])

    d0 = lax.broadcasted_iota(jnp.int32, (members, members), 0)
    d1 = lax.broadcasted_iota(jnp.int32, (members, members), 1)
    summed_up = blocks_out[...].reshape(members, 2 * members)
    system[:, 0:members] = summed_up[:, 0:members] + jnp.where(d0 == d1, float(members), 0.0)
    system[:, members:] = summed_up[:, members:]
    lane = lax.broadcasted_iota(jnp.int32, (1, 2 * members), 1)

    def eliminate(i, _):
        now = system[...]
        top = system[pl.ds(i, 1), :]
        col = jnp.sum(jnp.where(lane == i, now, 0.0), axis=1, keepdims=True)
        pivot = jnp.sum(jnp.where(lane == i, top, 0.0), axis=1, keepdims=True)
        top = top / pivot
        system[...] = now - col * top
        system[pl.ds(i, 1), :] = top
        return 0

    lax.fori_loop(0, members, eliminate, 0)
    gain = system[:, members:].astype(jnp.bfloat16)
    peers = GROUP // ROWS

    @pl.loop(0, count // GROUP)
    def _(g):
        ir = lax.broadcasted_iota(jnp.int32, (GROUP, members), 0) // ROWS + g * peers
        jj = lax.broadcasted_iota(jnp.int32, (GROUP, members), 1)
        pick = jnp.where(peer_at(me, ir) == jj, 1.0, 0.0).astype(jnp.bfloat16)
        spread_out = lax.dot_general(pick, gain, LAST, preferred_element_type=jnp.float32)
        out_rows = pl.ds(pl.multiple_of(g * GROUP, GROUP), GROUP)
        weight_sums[out_rows, :] = jnp.sum(spread_out, axis=1, keepdims=True)
        spread_out = spread_out.astype(jnp.bfloat16)

        @pl.loop(0, count // 512)
        def _(q):
            c = pl.ds(pl.multiple_of(q * 512, 512), 512)
            full = jnp.dot(spread_out, spread[:, c], preferred_element_type=jnp.float32)
            r0 = lax.broadcasted_iota(jnp.int32, (GROUP, 512), 0) % ROWS
            r1 = lax.broadcasted_iota(jnp.int32, (GROUP, 512), 1) % ROWS
            weights[out_rows, c] = jnp.where(r0 == r1, full, 0.0).astype(jnp.bfloat16)

    tr = lax.broadcasted_iota(jnp.int32, (ROWS, count), 1) % ROWS
    tw = lax.broadcasted_iota(jnp.int32, (ROWS, count), 0)
    same = jnp.where(tr == tw, 1.0, 0.0).astype(jnp.bfloat16)

    def mean_of(c):
        avg[:, c] = jnp.dot(same, slab[:, c], preferred_element_type=jnp.float32) * (1.0 / members)

    def mix(g, c, width):
        out_rows = pl.ds(pl.multiple_of(g * GROUP, GROUP), GROUP)
        acc = jnp.dot(weights[out_rows, :], slab[:, c], preferred_element_type=jnp.float32)
        means = jnp.broadcast_to(avg[:, c][None], (peers, ROWS, width)).reshape(GROUP, width)
        mixed[out_rows, c] = (acc - weight_sums[out_rows, :] * means).astype(jnp.bfloat16)

    def tiles(lo, hi, do):
        @pl.loop(lo // 256, hi // 256)
        def _(n):
            do(pl.ds(pl.multiple_of(n * 256, 256), 256))

    targets = (
        (cols_near, new_second.at[mine, left_half]),
        (cols_first, new_first.at[first_part(me)]),
        (cols_far, new_second.at[mine, right_half]),
        (cols_extra, new_third.at[third_part(tile)]),
        (cols_extra, bias_back),
    )

    def send_back(i, k):
        c, dst = targets[k]
        send = back_send.at[k]
        remote(mixed.at[rows_of(i), c], dst, send, back_recv.at[k], peer_at(me, i)).start()

    def keep_own(k):
        c, dst = targets[k]
        pltpu.make_async_copy(mixed.at[pl.ds(0, ROWS), c], dst, back_recv.at[k]).start()

    def mix_and_send(early):
        def send(i):
            for k in (0, 1) if early else (2,):
                send_back(i, k)
            if not early:
                pl.when(holds)(lambda: send_back(i, 3))
                pl.when(me == BIAS_AT)(lambda: send_back(i, 4))

        @pl.loop(0, count // GROUP)
        def _(g):
            if early:
                tiles(0, near + narrow, lambda c: mix(g, c, 256))
            else:
                tiles(near + narrow, main, lambda c: mix(g, c, 256))
                pl.when(extra_here)(lambda: mix(g, cols_extra, LANES))

            @pl.loop(jnp.where(g == 0, 1, g * peers), (g + 1) * peers)
            def _(i):
                send(i)

        for k in (0, 1) if early else (2,):
            keep_own(k)
        if not early:
            pl.when(holds)(lambda: keep_own(3))
            pl.when(me == BIAS_AT)(lambda: keep_own(4))

    drain(slab.at[:, cols_early], recv_sem.at[0])
    tiles(0, near + narrow, mean_of)
    mix_and_send(True)
    drain(slab.at[:, cols_far], recv_sem.at[1])
    pl.when(extra_here)(lambda: drain(slab.at[:, cols_extra], recv_extra))
    tiles(near + narrow, main, mean_of)
    pl.when(extra_here)(lambda: mean_of(cols_extra))
    mix_and_send(False)

    others = pl.ds(0, (members - 1) * ROWS)
    for u in range(units):
        sent_unit(u)
    drain(outgoing, small_send.at[0])
    for k in (2, 5):
        drain(moments.at[pl.ds(0, planes - 1)], small_send.at[k])
    for k in (3, 4):
        drain(block, small_send.at[k])

    @pl.when(extra_here)
    def _():
        drain(slab.at[pl.ds(0, THIRDS * ROWS), cols_extra], send_extra)

    @pl.when(jnp.logical_not(extra_here))
    def _():
        drain(slab.at[pl.ds(0, (THIRDS + 1) * ROWS), cols_extra], send_extra)

    for k in range(3):
        drain(mixed.at[others, targets[k][0]], back_send.at[k])
    pl.when(holds)(lambda: drain(mixed.at[others, cols_extra], back_send.at[3]))
    pl.when(me == BIAS_AT)(lambda: drain(mixed.at[others, cols_extra], back_send.at[4]))
    drain(new_second.at[:, left_half], back_recv.at[0])
    drain(new_first, back_recv.at[1])
    drain(bias_back, back_recv.at[4])
    bias_wide[...] = bias_back[...].astype(jnp.float32)
    for i in range(8):
        c = slice(i * LANES, (i + 1) * LANES)
        new_bfirst[:, c] = bias_wide[i : i + 1, :].astype(jnp.bfloat16)
        new_bsecond[:, c] = bias_wide[8 + i : 9 + i, :].astype(jnp.bfloat16)
    drain(new_third, back_recv.at[3])
    drain(new_second.at[:, right_half], back_recv.at[2])


def store_kernel(*refs):
    n = (len(refs) - 1) // 2
    sem = refs[-1]
    copies = []
    for src, dst in zip(refs[:n], refs[n : 2 * n]):
        cuts = max(1, src.shape[0] // 512)
        rows = src.shape[0] // cuts
        for k in range(cuts):
            at = pl.ds(k * rows, rows)
            copies.append(
                pltpu.make_async_copy(src.at[at, :], dst.at[at, :], sem.at[len(copies)])
            )
    for copy in copies:
        copy.start()
    for copy in copies:
        copy.wait()


def body(samples, w_first, b_first, w_second, b_second, w_third, observed, perturb, variance):
    members = lax.axis_size("member")
    in_scale = samples.shape[1] ** (-0.5)
    hid_scale = w_second.shape[1] ** (-0.5)
    first_w, second_w, third_w = w_first[0], w_second[0], w_third[0].T
    count = members * ROWS
    wide = second_w.shape[1] + first_w.shape[1] // 4 + LANES
    batch, hidden, outs = samples.shape[0], second_w.shape[1], third_w.shape[0]
    anywhere = pl.BlockSpec(memory_space=pl.ANY)
    onchip = pl.BlockSpec(memory_space=pltpu.VMEM)
    dma = pltpu.SemaphoreType.DMA
    low, full = jnp.bfloat16, jnp.float32
    by_plane = (members // RING, RING, 2 * LANES)
    shapes = (first_w, b_first, second_w, b_second, third_w)
    mixed = pl.pallas_call(
        functools.partial(kernel, members, in_scale, hid_scale),
        out_shape=[pltpu.VMEM(a.shape, a.dtype) for a in shapes],
        in_specs=[anywhere] * 9,
        out_specs=[onchip] * 5,
        scratch_shapes=[
            pltpu.VMEM((count, wide), low),
            pltpu.VMEM((count, wide), low),
            pltpu.VMEM((count, count), low),
            pltpu.VMEM((count, 1), full),
            pltpu.VMEM((members, count), low),
            pltpu.VMEM((ROWS, wide), full),
            pltpu.VMEM(samples.shape, low),
            pltpu.VMEM(first_w.shape, low),
            pltpu.VMEM(second_w.shape, low),
            pltpu.VMEM(third_w.shape, low),
            pltpu.VMEM(b_first.shape, low),
            pltpu.VMEM(b_second.shape, low),
            pltpu.VMEM((outs, batch // 2), full),
            pltpu.VMEM((outs, batch // 2), full),
            pltpu.VMEM((outs, batch // 2), full),
            pltpu.VMEM((batch, hidden), low),
            pltpu.VMEM((batch, hidden), low),
            pltpu.VMEM((batch, hidden), low),
            pltpu.VMEM((outs, batch), full),
            pltpu.VMEM((outs, batch // 2), full),
            pltpu.VMEM((members, 2 * LANES), full),
            pltpu.VMEM((members, 2 * LANES), full),
            pltpu.VMEM(by_plane, full),
            pltpu.VMEM(by_plane, full),
            pltpu.VMEM((RING, 2 * LANES), full),
            pltpu.VMEM((RING, 2 * LANES), full),
            pltpu.VMEM((1, 2 * LANES), full),
            pltpu.VMEM((1, 2 * LANES), full),
            pltpu.VMEM((RING, 2 * LANES), full),
            pltpu.VMEM(by_plane, full),
            pltpu.VMEM((members, 2 * LANES), full),
            pltpu.VMEM((1, 2 * LANES), full),
            pltpu.VMEM((1, 2 * LANES), full),
            pltpu.VMEM((1, 2 * LANES), full),
            pltpu.VMEM((ROWS, LANES), full),
            pltpu.VMEM((ROWS, LANES), low),
            pltpu.VMEM((ROWS, LANES), low),
            dma((9,)),
            dma((2 * members // PACE,)),
            dma((2,)),
            dma,
            dma,
            dma((3,)),
            dma((3,)),
            dma((6,)),
            dma((6,)),
            dma((5,)),
            dma((5,)),
        ],
        compiler_params=pltpu.CompilerParams(
            collective_id=0, has_side_effects=True, vmem_limit_bytes=50 << 20
        ),
    )(
        *(
            pltpu.with_memory_space_constraint(a, pltpu.HBM)
            for a in (
                samples,
                first_w,
                b_first,
                second_w,
                b_second,
                third_w,
                observed.T,
                perturb[0].T,
                variance.T,
            )
        )
    )
    new_first, new_bfirst, new_second, new_bsecond, new_third = pl.pallas_call(
        store_kernel,
        out_shape=[jax.ShapeDtypeStruct(a.shape, a.dtype) for a in shapes],
        in_specs=[anywhere] * 5,
        out_specs=[anywhere] * 5,
        scratch_shapes=[dma((8,))],
        compiler_params=pltpu.CompilerParams(vmem_limit_bytes=1 << 20),
    )(*(pltpu.with_memory_space_constraint(a, pltpu.VMEM) for a in mixed))
    return (new_first[None], new_bfirst, new_second[None], new_bsecond, new_third.T[None])


def solution(mesh):
    in_specs = (
        P(),
        P("member", None, "pair"),
        P("member", "pair"),
        P("member", None, "pair"),
        P("member", "pair"),
        P("member", "pair", None),
        P(),
        P("member", None, None),
        P(),
    )
    out_specs = (
        P("member", None, "pair"),
        P("member", "pair"),
        P("member", None, "pair"),
        P("member", "pair"),
        P("member", "pair", None),
    )
    return jax.shard_map(body, mesh=mesh, in_specs=in_specs, out_specs=out_specs, check_vma=False)
```
